32 devices in a mesh: dom: 4 (over z), lev: 4 (over y, x), mem: 2 (over core).
Axes of the slice: x: 2, y: 2, z: 4, core: 2. Of those that a mesh axis runs over, the one named last changes fastest.
Arguments:
- node_state: bfloat16 [2, 4, 32, 128, 128], P('mem', 'lev', 'dom'), may hold values from -6 to 6
- state_cotangent: bfloat16 [2, 4, 32, 128, 128], P('mem', 'lev', 'dom'), may hold values from -6 to 6
- edge_first: bfloat16 [256, 128], replicated, may hold values from -0.375 to 0.375
- edge_second: bfloat16 [128, 128], replicated, may hold values from -0.5 to 0.5
- node_first: bfloat16 [384, 128], replicated, may hold values from -0.3125 to 0.3125
- node_second: bfloat16 [128, 128], replicated, may hold values from -0.5 to 0.5
- inner_count: int32 [4], P('dom'), may hold values from 8 to 16, as said below
- inner_pairs: int32 [64, 2], P('dom'), may hold values from 0 to 7, as said below
- outer_pairs: int32 [32, 2], P('dom'), may hold values from 0 to 3
Outputs:
- updated: bfloat16 [2, 4, 32, 128, 128], P('mem', 'lev', 'dom')
- state_grad: bfloat16 [2, 4, 32, 128, 128], P('mem', 'lev', 'dom')
- edge_first_grad: float32 [256, 128], replicated
- edge_second_grad: float32 [128, 128], replicated
- node_first_grad: float32 [384, 128], replicated
- node_second_grad: float32 [128, 128], replicated
The draws below stay inside these ranges and needn't reach their ends.
Inputs may be any that keep to these rules, and one draw needn't show every extreme that they name: `inner_count`: every entry lies between 8 and 16; some partition has exactly 16 live slots and some exactly 8; slots at and past the count hold valid block pairs that carry no flux. `inner_pairs`: the two block indices of a slot differ.
All inputs are finite; a program needn't handle non-finite values.
Results may differ from the reference program's by a relative error of at most 0.008.
Values may be sent and summed in bfloat16 or wider, within the bound.
A program may use at most 64 MiB of HBM per device.

```python
import math
import jax
import jax.numpy as jnp
from jax import lax

H = 128
BLK = 128
NB = 8
BND = 4
FO = 4
REACH = 2
FI = 16
NBLK = 32
LEVELS = 4
ENS = 2
N_DOM = 4


def draw_inner_count(key, part):
    first_key, second_key, third_key = jax.random.split(key, 3)
    counts = jax.random.randint(first_key, (N_DOM,), NB, FI + 1)
    top_pick = jax.random.randint(second_key, (), 0, N_DOM)
    low_pick = (top_pick + 1 + jax.random.randint(third_key, (), 0, N_DOM - 1)) % N_DOM
    places = jnp.arange(N_DOM, dtype=jnp.int32)
    counts = jnp.where(places == top_pick, FI, counts)
    counts = jnp.where(places == low_pick, NB, counts)
    return counts.astype(jnp.int32)


def draw_inner_pairs(key, part):
    first_key, second_key = jax.random.split(key)
    left_block = jax.random.randint(first_key, (N_DOM * FI,), 0, NB)
    step_block = jax.random.randint(second_key, (N_DOM * FI,), 1, NB)
    right_block = (left_block + step_block) % NB
    return jnp.stack([left_block, right_block], axis=1).astype(jnp.int32)


def with_ends(result, key, smallest, largest):
    longest = result.shape.index(max(result.shape))
    spots = []
    for shift in (0, 1):
        where = [jax.random.randint(jax.random.fold_in(key, axis), (), 0, length) for axis, length in enumerate(result.shape)]
        where[longest] = (where[longest] + shift) % result.shape[longest]
        spots.append(tuple(where))
    return result.at[spots[0]].set(smallest).at[spots[1]].set(largest)


def level_of(stream_key, shape, cuts, least, high):
    loudness = 1.0
    for position, blocks in cuts:
        steps = jax.random.uniform(jax.random.fold_in(jax.random.fold_in(stream_key, 6), position), (blocks,), jnp.float32, least / len(cuts), high / len(cuts))
        loudness = loudness * jnp.repeat(jnp.exp(steps), shape[position] // blocks).reshape((-1,) + (1,) * (len(shape) - 1 - position))
    return loudness


def normal_values(stream_key, dims, width, bound, cuts=(), held_as=jnp.bfloat16):
    result = width * jax.random.normal(stream_key, dims, jnp.float32)
    if cuts:
        result = result * level_of(stream_key, dims, cuts, -0.22, 0.18)
    return jnp.clip(result, -bound, bound).astype(held_as)


def setup_inputs(seed: int = 0) -> dict:
    key_list = jax.random.split(jax.random.key(seed), 10)
    node_state = normal_values(key_list[0], (ENS, LEVELS, NBLK, BLK, H), 1.0, 6.0, ((0, 2), (1, 4), (2, 4)))
    state_cotangent = normal_values(key_list[1], (ENS, LEVELS, NBLK, BLK, H), 1.0, 6.0, ((0, 2), (1, 4), (2, 4)))
    edge_first = normal_values(key_list[2], (2 * H, H), (2 * H) ** -0.5, 0.375)
    edge_second = normal_values(key_list[3], (H, H), H ** -0.5, 0.5)
    node_first = normal_values(key_list[4], (3 * H, H), (3 * H) ** -0.5, 0.3125)
    node_second = normal_values(key_list[5], (H, H), H ** -0.5, 0.5)
    inner_count = draw_inner_count(jax.random.fold_in(key_list[9], 71), 0)
    inner_pairs = draw_inner_pairs(jax.random.fold_in(key_list[9], 71), 0)
    outer_pairs = with_ends(jax.random.randint(key_list[8], (N_DOM * REACH * FO, 2), 0, BND), jax.random.fold_in(key_list[8], 1), 0, BND - 1).astype(jnp.int32)
    return dict(node_state=node_state, state_cotangent=state_cotangent, edge_first=edge_first, edge_second=edge_second, node_first=node_first, node_second=node_second, inner_count=inner_count, inner_pairs=inner_pairs, outer_pairs=outer_pairs)


precise_mode = lax.Precision.HIGHEST

def swish_slope(pre_value):
    sigmoid_val = jax.nn.sigmoid(pre_value)
    return sigmoid_val * (1.0 + pre_value * (1.0 - sigmoid_val))

def mixed_product(form, first, second):
    return jnp.einsum(form, first.astype(jnp.float32), second.astype(jnp.float32), precision=precise_mode)

def edge_terms(left_rows, right_rows, edge_first, edge_second):
    inputs = jnp.stack([jnp.concatenate([left_rows, right_rows], -1), jnp.concatenate([right_rows, left_rows], -1)])
    pre_act = mixed_product('sfnk,kj->sfnj', inputs, edge_first)
    hidden = jax.nn.silu(pre_act).astype(jnp.bfloat16)
    phi_out = mixed_product('sfnk,kj->sfnj', hidden, edge_second)
    return (phi_out[0] - phi_out[1], inputs, pre_act, hidden)

def reference(node_state, state_cotangent, edge_first, edge_second, node_first, node_second, inner_count, inner_pairs, outer_pairs):
    parts = jnp.arange(N_DOM, dtype=jnp.int32)
    inner = inner_pairs.reshape(N_DOM, FI, 2)
    outer = outer_pairs.reshape(N_DOM, REACH, FO, 2)
    base_block = (parts * NB)[:, None]
    inner_left = inner[:, :, 0] + base_block
    inner_right = inner[:, :, 1] + base_block
    inner_live = (jnp.arange(FI, dtype=jnp.int32)[None, :] < inner_count[:, None]).astype(jnp.float32)
    partner = (parts[:, None] + jnp.arange(1, REACH + 1, dtype=jnp.int32)[None, :]) % N_DOM
    outer_left = outer[..., 0] + base_block[:, :, None]
    outer_right = outer[..., 1] + (partner * NB)[:, :, None]
    face_left = jnp.concatenate([inner_left, outer_left.reshape(N_DOM, REACH * FO)], 1).astype(jnp.int32)
    face_right = jnp.concatenate([inner_right, outer_right.reshape(N_DOM, REACH * FO)], 1).astype(jnp.int32)
    face_live = jnp.concatenate([inner_live, jnp.ones((N_DOM, REACH * FO), jnp.float32)], 1)
    flat_state = node_state.reshape(ENS * LEVELS, NBLK, BLK, H)
    flat_cot = state_cotangent.reshape(ENS * LEVELS, NBLK, BLK, H)

    def level_flux(level_state):

        def part_flux(face_group):
            left_idx, right_idx, live = face_group
            face_flux = edge_terms(level_state[left_idx], level_state[right_idx], edge_first, edge_second)[0]
            return face_flux * live[:, None, None]
        face_flux = lax.map(part_flux, (face_left, face_right, face_live)).reshape(-1, BLK, H)
        node_flux = jnp.zeros((NBLK, BLK, H), jnp.float32)
        node_flux = node_flux.at[face_left.reshape(-1)].add(face_flux)
        return node_flux.at[face_right.reshape(-1)].add(-face_flux)
    node_flux = lax.map(level_flux, flat_state)
    depth_sum = lax.optimization_barrier(jnp.sum(node_flux.reshape(ENS, LEVELS, NBLK, BLK, H), axis=1))
    depth_mean = (depth_sum / LEVELS).astype(jnp.bfloat16)
    mean_flat = jnp.repeat(depth_mean, LEVELS, axis=0)

    def node_step(node_args):
        level_state, level_flux_val, level_mean, level_cot = node_args
        joined = jnp.concatenate([level_state, level_flux_val.astype(jnp.bfloat16), level_mean], -1)
        node_pre = mixed_product('bnk,kj->bnj', joined, node_first)
        node_hidden = jax.nn.silu(node_pre).astype(jnp.bfloat16)
        new_state = (level_state.astype(jnp.float32) + mixed_product('bnk,kj->bnj', node_hidden, node_second)).astype(jnp.bfloat16)
        node_grad = (mixed_product('bnj,kj->bnk', level_cot, node_second) * swish_slope(node_pre)).astype(jnp.bfloat16)
        joined_grad = mixed_product('bnj,kj->bnk', node_grad, node_first)
        grad_first = mixed_product('bnk,bnj->kj', joined, node_grad)
        grad_second = mixed_product('bnk,bnj->kj', node_hidden, level_cot)
        state_part = level_cot.astype(jnp.float32) + joined_grad[..., :H]
        return (new_state, state_part, joined_grad[..., H:2 * H], joined_grad[..., 2 * H:], grad_first, grad_second)
    new_state, state_part, flux_part, mean_part, node_first_terms, node_second_terms = lax.map(node_step, (flat_state, node_flux, mean_flat, flat_cot))
    mean_sum = lax.optimization_barrier(jnp.sum(mean_part.reshape(ENS, LEVELS, NBLK, BLK, H), axis=1))
    mean_grad = (mean_sum / LEVELS).astype(jnp.bfloat16)
    flux_grad_node = flux_part + jnp.repeat(mean_grad.astype(jnp.float32), LEVELS, axis=0)

    def level_back(back_args):
        level_state, level_grad = back_args

        def part_back(face_group):
            left_idx, right_idx, live = face_group
            face_flux, inputs, pre_act, hidden = edge_terms(level_state[left_idx], level_state[right_idx], edge_first, edge_second)
            face_grad = ((level_grad[left_idx] - level_grad[right_idx]) * live[:, None, None]).astype(jnp.bfloat16)
            signed = jnp.stack([face_grad, -face_grad])
            pre_grad = (mixed_product('sfnj,kj->sfnk', signed, edge_second) * swish_slope(pre_act)).astype(jnp.bfloat16)
            grad_second = mixed_product('sfnk,sfnj->kj', hidden, signed)
            grad_first = mixed_product('sfnk,sfnj->kj', inputs, pre_grad)
            input_grad = mixed_product('sfnj,kj->sfnk', pre_grad, edge_first)
            left_grad = input_grad[0, ..., :H] + input_grad[1, ..., H:]
            right_grad = input_grad[0, ..., H:] + input_grad[1, ..., :H]
            return (left_grad, right_grad, grad_first, grad_second)
        left_grad, right_grad, grad_first, grad_second = lax.map(part_back, (face_left, face_right, face_live))
        edge_part = jnp.zeros((NBLK, BLK, H), jnp.float32)
        edge_part = edge_part.at[face_left.reshape(-1)].add(left_grad.reshape(-1, BLK, H))
        edge_part = edge_part.at[face_right.reshape(-1)].add(right_grad.reshape(-1, BLK, H))
        return (edge_part, lax.optimization_barrier(jnp.sum(grad_first, axis=0)), lax.optimization_barrier(jnp.sum(grad_second, axis=0)))
    edge_part, edge_first_terms, edge_second_terms = lax.map(level_back, (flat_state, flux_grad_node))
    state_grad = (state_part + edge_part).astype(jnp.bfloat16).reshape(ENS, LEVELS, NBLK, BLK, H)
    grad_scale = 1.0 / math.sqrt(ENS * LEVELS * NBLK * BLK)
    return (new_state.reshape(ENS, LEVELS, NBLK, BLK, H), state_grad, lax.optimization_barrier(jnp.sum(edge_first_terms, axis=0)) * grad_scale, lax.optimization_barrier(jnp.sum(edge_second_terms, axis=0)) * grad_scale, lax.optimization_barrier(jnp.sum(node_first_terms, axis=0)) * grad_scale, lax.optimization_barrier(jnp.sum(node_second_terms, axis=0)) * grad_scale)
```

```python
import functools
import math

import jax
import jax.numpy as jnp
from jax import lax
from jax.experimental import pallas as pl
from jax.experimental.pallas import tpu as pltpu
from jax.sharding import PartitionSpec as P

BND = 4
REACH = 2
CHUNKS = 2
FWD_TILE = 32
BWD_TILE = 16
MESH = pl.DeviceIdType.MESH
F32 = jnp.float32
BF16 = jnp.bfloat16


def mm(a, b):
    return jnp.dot(a, b, preferred_element_type=F32)


def mm_nt(a, b):
    return lax.dot_general(a, b, (((1,), (1,)), ((), ())), preferred_element_type=F32)


def mm_tn(a, b):
    return lax.dot_general(a, b, (((0,), (0,)), ((), ())), preferred_element_type=F32)


def gate(z):
    return 0.5 * jnp.tanh(0.5 * z) + 0.5


def layer_kernel(
    sizes,
    offs,
    scale,
    count_ref,
    inner_ref,
    outer_ref,
    near1_ref,
    near2_ref,
    state_ref,
    cot_ref,
    ef_ref,
    es_ref,
    nf_ref,
    ns_ref,
    upd_ref,
    sgrad_ref,
    efg_ref,
    esg_ref,
    nfg_ref,
    nsg_ref,
    wd_s,
    wa_s,
    wc_s,
    wo_s,
    halo,
    tab,
    slope,
    nd,
    fluxb,
    frecv,
    meanb,
    pre,
    cotg,
    mpart,
    mrecv,
    mgrad,
    fpart,
    gw,
    gwsend,
    gwhalo,
    acc_a,
    acc_b,
    wacc,
    wsend,
    wrecv_n,
    wrecv_e,
    wdom_n,
    wdom_e,
    wfin,
    halo_ss,
    halo_rs,
    rs1_ss,
    rs1_rs,
    ag1_ss,
    ag1_rs,
    rs2_ss,
    rs2_rs,
    ag2_ss,
    ag2_rs,
    back_ss,
    back_rs,
    wr_ss,
    wr_rs,
    wd_ss,
    wd_rs,
    wg_ss,
    wg_rs,
):
    n_dom, n_lev, n_mem = sizes
    n_grp = n_lev * n_mem
    blocks, rows, h = state_ref.shape
    inner = inner_ref.shape[0]
    per = outer_ref.shape[0] // REACH
    chunk = rows // CHUNKS
    share = blocks // n_lev
    dom = lax.axis_index("dom")
    lev = lax.axis_index("lev")
    mem = lax.axis_index("mem")
    grp = lev * n_mem + mem

    def dom_dev(o):
        return {"dom": lax.rem(dom + o, n_dom), "lev": lev, "mem": mem}

    def lev_dev(k):
        return {"dom": dom, "lev": lax.rem(lev + k, n_lev), "mem": mem}

    def grp_id(k):
        return lax.rem(grp + k, n_grp)

    def grp_dev(k):
        g = grp_id(k)
        return {"dom": dom, "lev": g // n_mem, "mem": lax.rem(g, n_mem)}

    def remote(src, dst, ss, rs, dev):
        copy = pltpu.make_async_remote_copy(
            src_ref=src, dst_ref=dst, send_sem=ss, recv_sem=rs, device_id=dev, device_id_type=MESH
        )
        copy.start()
        return copy

    barrier = pltpu.get_barrier_semaphore()
    for o in range(1, n_dom):
        pl.semaphore_signal(barrier, inc=1, device_id=dom_dev(o), device_id_type=MESH)
    for k in range(1, n_grp):
        pl.semaphore_signal(barrier, inc=1, device_id=grp_dev(k), device_id_type=MESH)

    live = count_ref[0]
    for f in range(inner):
        m = jnp.where(f < live, 1.0, 0.0).astype(F32)
        a, c = inner_ref[f, 0], inner_ref[f, 1]
        for b in range(blocks):
            wa = jnp.where(a == b, m, 0.0)
            wc = jnp.where(c == b, m, 0.0)
            wa_s[f * blocks + b] = wa
            wc_s[f * blocks + b] = wc
            wd_s[f * blocks + b] = wa - wc
    outer = []
    for o in range(1, REACH + 1):
        near = near1_ref if o == 1 else near2_ref
        ahead = blocks + BND * offs.index(o % n_dom)
        behind = blocks + BND * offs.index(-o % n_dom)
        for j in range(per):
            outer.append((outer_ref[(o - 1) * per + j, 0], ahead + outer_ref[(o - 1) * per + j, 1]))
            outer.append((near[j, 1], behind + near[j, 0]))
    for f, (a, _) in enumerate(outer):
        for b in range(BND):
            wo_s[f * BND + b] = jnp.where(a == b, 1.0, 0.0).astype(F32)

    pl.semaphore_wait(barrier, n_dom - 1 + n_grp - 1)

    halo_c = []
    for c in range(CHUNKS):
        rc = pl.ds(c * chunk, chunk)
        halo_c.append(
            [
                remote(
                    state_ref.at[pl.ds(0, BND), rc],
                    halo.at[c, s],
                    halo_ss.at[c * len(offs) + s],
                    halo_rs.at[c * len(offs) + s],
                    dom_dev(n_dom - o),
                )
                for s, o in enumerate(offs)
            ]
        )

    ef_wide = jnp.concatenate([ef_ref[:h], ef_ref[h:]], axis=1)
    es = es_ref[...]
    ns = ns_ref[...]
    n0, n1, n2 = nf_ref[:h], nf_ref[h : 2 * h], nf_ref[2 * h :]

    def pair(f, ia, ic, at, size):
        ta = tab[ia, pl.ds(at, size), :]
        tc = tab[ic, pl.ds(at, size), :]
        z1 = ta[:, :h] + tc[:, h:]
        z2 = tc[:, :h] + ta[:, h:]
        g1, g2 = gate(z1), gate(z2)
        s1, s2 = z1 * g1, z2 * g2
        slope[f, 0, pl.ds(at, size), :] = g1 + s1 - s1 * g1
        slope[f, 1, pl.ds(at, size), :] = g2 + s2 - s2 * g2
        return s1 - s2

    def sum_faces(start, faces, table, width, base, at, size, load):
        acc = [nd[b, pl.ds(at, size), :] if load else None for b in range(width)]
        for f, (ia, ic) in enumerate(faces):
            d = pair(start + f, ia, ic, at, size)
            for b in range(width):
                term = table[f * width + b] * d
                acc[b] = term if acc[b] is None else acc[b] + term
        for b in range(width):
            nd[b, pl.ds(at, size), :] = acc[b]

    def tiles(c, size, body):
        def step(t, carry):
            body(pl.multiple_of(c * chunk + t * size, size))
            return carry

        lax.fori_loop(0, chunk // size, step, 0)

    def rows_of(ref, c):
        return ref[:, c * chunk : (c + 1) * chunk].reshape(-1, h)

    def put_rows(ref, c, value):
        ref[:, c * chunk : (c + 1) * chunk] = value.reshape(-1, chunk, value.shape[-1])

    inner_faces = [(inner_ref[f, 0], inner_ref[f, 1]) for f in range(inner)]
    for c in range(CHUNKS):
        tab[:blocks, c * chunk : (c + 1) * chunk] = mm(rows_of(state_ref, c), ef_wide).reshape(
            blocks, chunk, 2 * h
        )
        put_rows(cotg, c, mm_nt(rows_of(cot_ref, c), ns))
        put_rows(pre, c, mm(rows_of(state_ref, c), n0))
        tiles(
            c,
            FWD_TILE,
            lambda at: sum_faces(0, inner_faces, wd_s, blocks, 0, at, FWD_TILE, False),
        )

    def scatter(src, dst, ss, rs, c):
        out = []
        for k in range(1, n_lev):
            to = lax.rem(lev + k, n_lev)
            out.append(
                remote(
                    src.at[c, pl.ds(to * share, share)],
                    dst.at[c, k - 1],
                    ss.at[c * (n_lev - 1) + k - 1],
                    rs.at[c * (n_lev - 1) + k - 1],
                    lev_dev(k),
                )
            )
        return out

    def reduce_spread(copies, src, got, dst, ss, rs, c):
        for copy in copies:
            copy.wait_recv()
        mine = pl.ds(lev * share, share)
        total = src[c, mine].astype(F32)
        for k in range(n_lev - 1):
            total = total + got[c, k].astype(F32)
        dst[c, mine] = (total * (1.0 / n_lev)).astype(BF16)
        return [
            remote(
                dst.at[c, mine],
                dst.at[c, mine],
                ss.at[c * (n_lev - 1) + k - 1],
                rs.at[c * (n_lev - 1) + k - 1],
                lev_dev(k),
            )
            for k in range(1, n_lev)
        ]

    rs1 = []
    for c in range(CHUNKS):
        for copy in halo_c[c]:
            copy.wait_recv()
        tab[blocks:, c * chunk : (c + 1) * chunk] = mm(
            halo[c].reshape(-1, h), ef_wide
        ).reshape(-1, chunk, 2 * h)
        tiles(
            c,
            FWD_TILE,
            lambda at: sum_faces(inner, outer, wo_s, BND, 0, at, FWD_TILE, True),
        )
        fluxb[c] = mm(rows_of(nd, c).astype(BF16), es).astype(BF16).reshape(blocks, chunk, h)
        rs1.append(scatter(fluxb, frecv, rs1_ss, rs1_rs, c))
    ag1 = []
    for c in range(CHUNKS):
        put_rows(pre, c, rows_of(pre, c) + mm(fluxb[c].reshape(-1, h), n1))
        ag1.append(reduce_spread(rs1[c], fluxb, frecv, meanb, ag1_ss, ag1_rs, c))
    rs2 = []
    for c in range(CHUNKS):
        for copy in ag1[c]:
            copy.wait_recv()
        mean = meanb[c].reshape(-1, h)
        z = rows_of(pre, c) + mm(mean, n2)
        g = gate(z)
        s = z * g
        hidden = s.astype(BF16)
        grad = (rows_of(cotg, c) * (g + s - s * g)).astype(BF16)
        mpart[c] = mm_nt(grad, n2).astype(BF16).reshape(blocks, chunk, h)
        rs2.append(scatter(mpart, mrecv, rs2_ss, rs2_rs, c))
        state = rows_of(state_ref, c)
        cot = rows_of(cot_ref, c)
        put_rows(upd_ref, c, (state.astype(F32) + mm(hidden, ns)).astype(BF16))
        put_rows(pre, c, cot.astype(F32) + mm_nt(grad, n0))
        put_rows(fpart, c, mm_nt(grad, n1))
        parts = (
            mm_tn(state, grad),
            mm_tn(fluxb[c].reshape(-1, h), grad),
            mm_tn(mean, grad),
            mm_tn(hidden, cot),
        )
        for i, part in enumerate(parts):
            at = slice(i * h, (i + 1) * h)
            wacc[at] = part if c == 0 else wacc[at] + part
    ag2 = [
        reduce_spread(rs2[c], mpart, mrecv, mgrad, ag2_ss, ag2_rs, c) for c in range(CHUNKS)
    ]
    back = []
    for c in range(CHUNKS):
        for copy in ag2[c]:
            copy.wait_recv()
        grad = (rows_of(fpart, c) + mgrad[c].reshape(-1, h).astype(F32)).astype(BF16)
        wide = mm_nt(grad, es).reshape(blocks, chunk, h)
        gw[:blocks, c * chunk : (c + 1) * chunk] = wide
        gwsend[c] = wide[:BND].astype(BF16)
        back.append(
            [
                remote(
                    gwsend.at[c],
                    gwhalo.at[c, s],
                    back_ss.at[c * len(offs) + s],
                    back_rs.at[c * len(offs) + s],
                    dom_dev(n_dom - o),
                )
                for s, o in enumerate(offs)
            ]
        )
        part = mm_tn(rows_of(nd, c).astype(BF16), grad)
        at = slice(4 * h, 5 * h)
        wacc[at] = part if c == 0 else wacc[at] + part

    def weights_out(first, count, got, sem):
        size = count // n_grp
        wsend[first : first + count] = wacc[first : first + count].astype(BF16)
        return [
            remote(
                wsend.at[pl.ds(pl.multiple_of(first + grp_id(k) * size, 16), size)],
                got.at[k - 1],
                wr_ss.at[sem, k - 1],
                wr_rs.at[sem, k - 1],
                grp_dev(k),
            )
            for k in range(1, n_grp)
        ]

    def weights_mid(copies, first, count, got, held, sem):
        size = count // n_grp
        for copy in copies:
            copy.wait_recv()
        total = wacc[pl.ds(pl.multiple_of(first + grp * size, 16), size)]
        for k in range(n_grp - 1):
            total = total + got[k].astype(F32)
        held[dom] = total.astype(BF16)
        return [
            remote(
                held.at[dom],
                held.at[dom],
                wd_ss.at[sem, o - 1],
                wd_rs.at[sem, o - 1],
                dom_dev(o),
            )
            for o in range(1, n_dom)
        ]

    def weights_in(copies, first, count, held, sem):
        size = count // n_grp
        for copy in copies:
            copy.wait_recv()
        total = held[0].astype(F32)
        for o in range(1, n_dom):
            total = total + held[o].astype(F32)
        mine = pl.ds(pl.multiple_of(first + grp * size, 16), size)
        wfin[mine] = total.astype(BF16)
        return [
            remote(
                wfin.at[mine],
                wfin.at[mine],
                wg_ss.at[sem, k - 1],
                wg_rs.at[sem, k - 1],
                grp_dev(k),
            )
            for k in range(1, n_grp)
        ]

    def spread_faces(start, faces, width, at, size, load):
        aa = [acc_a[b, pl.ds(at, size), :] if load else None for b in range(width)]
        bb = [acc_b[b, pl.ds(at, size), :] if load else None for b in range(width)]

        def put(total, term):
            return term if total is None else total + term

        for f, (ia, ic) in enumerate(faces):
            t = gw[ia, pl.ds(at, size), :] - gw[ic, pl.ds(at, size), :]
            p1 = t * slope[start + f, 0, pl.ds(at, size), :]
            p2 = t * slope[start + f, 1, pl.ds(at, size), :]
            for b in range(width):
                if load:
                    w = wo_s[f * width + b]
                    aa[b] = put(aa[b], w * p1)
                    bb[b] = put(bb[b], -w * p2)
                else:
                    wa, wc = wa_s[f * width + b], wc_s[f * width + b]
                    aa[b] = put(aa[b], wa * p1 - wc * p2)
                    bb[b] = put(bb[b], wc * p1 - wa * p2)
        for b in range(width):
            acc_a[b, pl.ds(at, size), :] = aa[b]
            acc_b[b, pl.ds(at, size), :] = bb[b]

    n_rows = 5 * h
    w1 = weights_out(0, n_rows, wrecv_n, 0)
    for c in range(CHUNKS):
        tiles(c, BWD_TILE, lambda at: spread_faces(0, inner_faces, blocks, at, BWD_TILE, False))
        if c == 0:
            w2 = weights_mid(w1, 0, n_rows, wrecv_n, wdom_n, 0)
    for c in range(CHUNKS):
        for copy in back[c]:
            copy.wait_recv()
        gw[blocks:, c * chunk : (c + 1) * chunk] = (
            gwhalo[c].reshape(-1, chunk, h).astype(F32)
        )
        tiles(c, BWD_TILE, lambda at: spread_faces(inner, outer, BND, at, BWD_TILE, True))
        a = rows_of(acc_a, c).astype(BF16)
        b = rows_of(acc_b, c).astype(BF16)
        state = rows_of(state_ref, c)
        for i, part in enumerate((mm_tn(state, a), mm_tn(state, b))):
            at = slice((5 + i) * h, (6 + i) * h)
            wacc[at] = part if c == 0 else wacc[at] + part
        if c == CHUNKS - 1:
            e1 = weights_out(n_rows, 2 * h, wrecv_e, 1)
            w3 = weights_in(w2, 0, n_rows, wdom_n, 0)
        total = rows_of(pre, c) + mm_nt(a, ef_ref[:h]) + mm_nt(b, ef_ref[h:])
        put_rows(sgrad_ref, c, total.astype(BF16))
    e2 = weights_mid(e1, n_rows, 2 * h, wrecv_e, wdom_e, 1)
    for copy in w3:
        copy.wait_recv()
    nfg_ref[...] = wfin[: 3 * h].astype(F32) * scale
    nsg_ref[...] = wfin[3 * h : 4 * h].astype(F32) * scale
    esg_ref[...] = wfin[4 * h : 5 * h].astype(F32) * scale
    e3 = weights_in(e2, n_rows, 2 * h, wdom_e, 1)
    for group in halo_c + rs1 + ag1 + rs2 + ag2 + back + [w1, w2, w3, e1, e2]:
        for copy in group:
            copy.wait_send()
    for copy in e3:
        copy.wait()
    efg_ref[...] = wfin[5 * h :].astype(F32) * scale


def shards(
    node_state,
    state_cotangent,
    edge_first,
    edge_second,
    node_first,
    node_second,
    inner_count,
    inner_pairs,
    outer_pairs,
):
    state = node_state[0, 0]
    cot = state_cotangent[0, 0]
    blocks, rows, h = state.shape
    n_dom, n_lev, n_mem = (lax.axis_size(x) for x in ("dom", "lev", "mem"))
    n_grp = n_lev * n_mem
    inner = inner_pairs.shape[0]
    outer = outer_pairs.shape[0]
    per = outer // REACH
    offs = sorted({s * o % n_dom for o in range(1, REACH + 1) for s in (1, -1)})
    near = []
    for o in range(1, REACH + 1):
        hops = [(i, (i + o) % n_dom) for i in range(n_dom)]
        near.append(lax.ppermute(outer_pairs[(o - 1) * per : o * per], "dom", hops))
    scale = 1.0 / math.sqrt(n_mem * n_lev * blocks * n_dom * rows)
    faces = inner + 2 * outer
    chunk = rows // CHUNKS
    share = blocks // n_lev
    slots = len(offs)
    table = blocks + BND * slots
    size_n = 5 * h // n_grp
    size_e = 2 * h // n_grp
    dma = pltpu.SemaphoreType.DMA
    lev_sems = [dma((CHUNKS * (n_lev - 1),))] * 8
    full = (blocks, rows, h)
    cut = (CHUNKS, blocks, chunk, h)
    smem = pl.BlockSpec(memory_space=pltpu.SMEM)
    vmem = pl.BlockSpec(memory_space=pltpu.VMEM)
    upd, sgrad, efg, esg, nfg, nsg = pl.pallas_call(
        functools.partial(layer_kernel, (n_dom, n_lev, n_mem), offs, scale),
        out_shape=(
            jax.ShapeDtypeStruct(full, BF16),
            jax.ShapeDtypeStruct(full, BF16),
            jax.ShapeDtypeStruct((2 * h, h), F32),
            jax.ShapeDtypeStruct((h, h), F32),
            jax.ShapeDtypeStruct((3 * h, h), F32),
            jax.ShapeDtypeStruct((h, h), F32),
        ),
        in_specs=[smem] * 5 + [vmem] * 6,
        out_specs=(vmem,) * 6,
        scratch_shapes=[
            pltpu.SMEM((inner * blocks,), F32),
            pltpu.SMEM((inner * blocks,), F32),
            pltpu.SMEM((inner * blocks,), F32),
            pltpu.SMEM((2 * outer * BND,), F32),
            pltpu.VMEM((CHUNKS, slots, BND, chunk, h), BF16),
            pltpu.VMEM((table, rows, 2 * h), F32),
            pltpu.VMEM((faces, 2, rows, h), F32),
            pltpu.VMEM(full, F32),
            pltpu.VMEM(cut, BF16),
            pltpu.VMEM((CHUNKS, n_lev - 1, share, chunk, h), BF16),
            pltpu.VMEM(cut, BF16),
            pltpu.VMEM(full, F32),
            pltpu.VMEM(full, F32),
            pltpu.VMEM(cut, BF16),
            pltpu.VMEM((CHUNKS, n_lev - 1, share, chunk, h), BF16),
            pltpu.VMEM(cut, BF16),
            pltpu.VMEM(full, F32),
            pltpu.VMEM((table, rows, h), F32),
            pltpu.VMEM((CHUNKS, BND, chunk, h), BF16),
            pltpu.VMEM((CHUNKS, slots, BND, chunk, h), BF16),
            pltpu.VMEM(full, F32),
            pltpu.VMEM(full, F32),
            pltpu.VMEM((7 * h, h), F32),
            pltpu.VMEM((7 * h, h), BF16),
            pltpu.VMEM((n_grp - 1, size_n, h), BF16),
            pltpu.VMEM((n_grp - 1, size_e, h), BF16),
            pltpu.VMEM((n_dom, size_n, h), BF16),
            pltpu.VMEM((n_dom, size_e, h), BF16),
            pltpu.VMEM((7 * h, h), BF16),
            dma((CHUNKS * slots,)),
            dma((CHUNKS * slots,)),
            *lev_sems,
            dma((CHUNKS * slots,)),
            dma((CHUNKS * slots,)),
            dma((2, n_grp - 1)),
            dma((2, n_grp - 1)),
            dma((2, n_dom - 1)),
            dma((2, n_dom - 1)),
            dma((2, n_grp - 1)),
            dma((2, n_grp - 1)),
        ],
        compiler_params=pltpu.CompilerParams(
            collective_id=0, has_side_effects=True, vmem_limit_bytes=56 * 1024 * 1024
        ),
    )(
        inner_count,
        inner_pairs,
        outer_pairs,
        *near,
        state,
        cot,
        edge_first,
        edge_second,
        node_first,
        node_second,
    )
    return (upd[None, None], sgrad[None, None], efg, esg, nfg, nsg)


def solution(mesh):
    data = P("mem", "lev", "dom", None, None)
    return jax.shard_map(
        shards,
        mesh=mesh,
        in_specs=(data, data, P(), P(), P(), P(), P("dom"), P("dom", None), P("dom", None)),
        out_specs=(data, data, P(), P(), P(), P()),
        check_vma=False,
    )
```

```python
import functools
import math

import jax
import jax.numpy as jnp
from jax import lax
from jax.experimental import pallas as pl
from jax.experimental.pallas import tpu as pltpu
from jax.sharding import PartitionSpec as P

BND = 4
REACH = 2
CHUNKS = 4
FWD_TILE = 32
BWD_TILE = 16
MESH = pl.DeviceIdType.MESH
F32 = jnp.float32
BF16 = jnp.bfloat16


def mm(a, b):
    return jnp.dot(a, b, preferred_element_type=F32)


def mm_nt(a, b):
    return lax.dot_general(a, b, (((1,), (1,)), ((), ())), preferred_element_type=F32)


def mm_tn(a, b):
    return lax.dot_general(a, b, (((0,), (0,)), ((), ())), preferred_element_type=F32)


def gate(z):
    return 0.5 * jnp.tanh(0.5 * z) + 0.5


def layer_kernel(
    sizes,
    offs,
    count_ref,
    inner_ref,
    outer_ref,
    state_any,
    cot_any,
    ef_any,
    es_any,
    nf_any,
    ns_any,
    upd_ref,
    sgrad_ref,
    wfin,
    near,
    wd_s,
    wa_s,
    wc_s,
    wo_s,
    halo,
    tab,
    slope,
    nd,
    fluxb,
    frecv,
    meanb,
    pre,
    cotg,
    hiddenb,
    gradb,
    fgradb,
    mpart,
    mrecv,
    mgrad,
    fpart,
    gw,
    gwsend,
    gwhalo,
    acc_a,
    acc_b,
    wacc,
    wsend,
    wrecv_n,
    wrecv_e,
    wdom_n,
    wdom_e,
    halo_ss,
    halo_rs,
    rs1_ss,
    rs1_rs,
    ag1_ss,
    ag1_rs,
    rs2_ss,
    rs2_rs,
    ag2_ss,
    ag2_rs,
    back_ss,
    back_rs,
    wr_ss,
    wr_rs,
    wd_ss,
    wd_rs,
    wg_ss,
    wg_rs,
    near_ss,
    near_rs,
    state_ref,
    cot_ref,
    ef_ref,
    es_ref,
    nf_ref,
    ns_ref,
    load_s,
):
    n_dom, n_lev, n_mem = sizes
    n_grp = n_lev * n_mem
    blocks, rows, h = state_ref.shape
    inner = inner_ref.shape[1]
    per = outer_ref.shape[1] // REACH
    chunk = rows // CHUNKS
    share = blocks // n_lev
    dom = lax.axis_index("dom")
    lev = lax.axis_index("lev")
    mem = lax.axis_index("mem")
    grp = lev * n_mem + mem

    def dom_dev(o):
        return {"dom": lax.rem(dom + o, n_dom), "lev": lev, "mem": mem}

    def lev_dev(k):
        return {"dom": dom, "lev": lax.rem(lev + k, n_lev), "mem": mem}

    def grp_id(k):
        return lax.rem(grp + k, n_grp)

    def grp_dev(k):
        g = grp_id(k)
        return {"dom": dom, "lev": g // n_mem, "mem": lax.rem(g, n_mem)}

    def remote(src, dst, ss, rs, dev):
        copy = pltpu.make_async_remote_copy(
            src_ref=src, dst_ref=dst, send_sem=ss, recv_sem=rs, device_id=dev, device_id_type=MESH
        )
        copy.start()
        return copy

    loads = []
    for i, (src, dst) in enumerate(
        (
            (state_any, state_ref),
            (ef_any, ef_ref),
            (cot_any, cot_ref),
            (ns_any, ns_ref),
            (nf_any, nf_ref),
            (es_any, es_ref),
        )
    ):
        load = pltpu.make_async_copy(src, dst, load_s.at[i])
        load.start()
        loads.append(load)

    barrier = pltpu.get_barrier_semaphore()
    for o in range(1, n_dom):
        pl.semaphore_signal(barrier, inc=1, device_id=dom_dev(o), device_id_type=MESH)
    for k in range(1, n_grp):
        pl.semaphore_signal(barrier, inc=1, device_id=grp_dev(k), device_id_type=MESH)

    live = count_ref[0]
    for f in range(inner):
        m = jnp.where(f < live, 1.0, 0.0).astype(F32)
        a, c = inner_ref[0, f], inner_ref[1, f]
        for b in range(blocks):
            wa = jnp.where(a == b, m, 0.0)
            wc = jnp.where(c == b, m, 0.0)
            wa_s[f * blocks + b] = wa
            wc_s[f * blocks + b] = wc
            wd_s[f * blocks + b] = wa - wc
    pl.semaphore_wait(barrier, n_dom - 1 + n_grp - 1)
    near_c = [
        remote(outer_ref, near.at[o - 1], near_ss.at[o - 1], near_rs.at[o - 1], dom_dev(o))
        for o in range(1, REACH + 1)
    ]

    halo_c = []
    for c in range(CHUNKS):
        rc = pl.ds(c * chunk, chunk)
        halo_c.append(
            [
                remote(
                    state_any.at[pl.ds(0, BND), rc],
                    halo.at[c, s],
                    halo_ss.at[c * len(offs) + s],
                    halo_rs.at[c * len(offs) + s],
                    dom_dev(n_dom - o),
                )
                for s, o in enumerate(offs)
            ]
        )

    for load in loads:
        load.wait()
    ef_wide = jnp.concatenate([ef_ref[:h], ef_ref[h:]], axis=1)
    es = es_ref[...]
    ns = ns_ref[...]
    n0, n1, n2 = nf_ref[:h], nf_ref[h : 2 * h], nf_ref[2 * h :]

    def pair(f, ia, ic, at, size):
        ta = tab[ia, pl.ds(at, size), :]
        tc = tab[ic, pl.ds(at, size), :]
        z1 = ta[:, :h] + tc[:, h:]
        z2 = tc[:, :h] + ta[:, h:]
        g1, g2 = gate(z1), gate(z2)
        s1, s2 = z1 * g1, z2 * g2
        slope[f, 0, pl.ds(at, size), :] = g1 + s1 - s1 * g1
        slope[f, 1, pl.ds(at, size), :] = g2 + s2 - s2 * g2
        return s1 - s2

    def sum_faces(start, faces, table, width, base, at, size, load):
        acc = [nd[b, pl.ds(at, size), :] if load else None for b in range(width)]
        for f, (ia, ic) in enumerate(faces):
            d = pair(start + f, ia, ic, at, size)
            for b in range(width):
                term = table[f * width + b] * d
                acc[b] = term if acc[b] is None else acc[b] + term
        for b in range(width):
            nd[b, pl.ds(at, size), :] = acc[b]

    def tiles(c, size, body):
        def step(t, carry):
            body(pl.multiple_of(c * chunk + t * size, size))
            return carry

        lax.fori_loop(0, chunk // size, step, 0)

    def rows_of(ref, c):
        return ref[:, c * chunk : (c + 1) * chunk].reshape(-1, h)

    def put_rows(ref, c, value):
        ref[:, c * chunk : (c + 1) * chunk] = value.reshape(-1, chunk, value.shape[-1])

    inner_faces = [(inner_ref[0, f], inner_ref[1, f]) for f in range(inner)]
    for c in range(CHUNKS):
        tab[:blocks, c * chunk : (c + 1) * chunk] = mm(rows_of(state_ref, c), ef_wide).reshape(
            blocks, chunk, 2 * h
        )
        put_rows(cotg, c, mm_nt(rows_of(cot_ref, c), ns))
        put_rows(pre, c, mm(rows_of(state_ref, c), n0))
        tiles(
            c,
            FWD_TILE,
            lambda at: sum_faces(0, inner_faces, wd_s, blocks, 0, at, FWD_TILE, False),
        )

    def scatter(src, dst, ss, rs, c):
        out = []
        for k in range(1, n_lev):
            to = lax.rem(lev + k, n_lev)
            out.append(
                remote(
                    src.at[c, pl.ds(to * share, share)],
                    dst.at[c, k - 1],
                    ss.at[c * (n_lev - 1) + k - 1],
                    rs.at[c * (n_lev - 1) + k - 1],
                    lev_dev(k),
                )
            )
        return out

    def reduce_spread(copies, src, got, dst, ss, rs, c):
        for copy in copies:
            copy.wait_recv()
        mine = pl.ds(lev * share, share)
        total = src[c, mine].astype(F32)
        for k in range(n_lev - 1):
            total = total + got[c, k].astype(F32)
        dst[c, mine] = (total * (1.0 / n_lev)).astype(BF16)
        return [
            remote(
                dst.at[c, mine],
                dst.at[c, mine],
                ss.at[c * (n_lev - 1) + k - 1],
                rs.at[c * (n_lev - 1) + k - 1],
                lev_dev(k),
            )
            for k in range(1, n_lev)
        ]

    for copy in near_c:
        copy.wait_recv()
    outer = []
    for o in range(1, REACH + 1):
        ahead = blocks + BND * offs.index(o % n_dom)
        behind = blocks + BND * offs.index(-o % n_dom)
        for j in range(per):
            i = (o - 1) * per + j
            outer.append((outer_ref[0, i], ahead + outer_ref[1, i]))
            outer.append((near[o - 1, 1, i], behind + near[o - 1, 0, i]))
    for f, (a, _) in enumerate(outer):
        for b in range(BND):
            wo_s[f * BND + b] = jnp.where(a == b, 1.0, 0.0).astype(F32)

    rs1 = []
    for c in range(CHUNKS):
        for copy in halo_c[c]:
            copy.wait_recv()
        tab[blocks:, c * chunk : (c + 1) * chunk] = mm(
            halo[c].reshape(-1, h), ef_wide
        ).reshape(-1, chunk, 2 * h)
        tiles(
            c,
            FWD_TILE,
            lambda at: sum_faces(inner, outer, wo_s, BND, 0, at, FWD_TILE, True),
        )
        fluxb[c] = mm(rows_of(nd, c).astype(BF16), es).astype(BF16).reshape(blocks, chunk, h)
        rs1.append(scatter(fluxb, frecv, rs1_ss, rs1_rs, c))
    ag1 = []
    for c in range(CHUNKS):
        put_rows(pre, c, rows_of(pre, c) + mm(fluxb[c].reshape(-1, h), n1))
        ag1.append(reduce_spread(rs1[c], fluxb, frecv, meanb, ag1_ss, ag1_rs, c))
    rs2 = []
    for c in range(CHUNKS):
        for copy in ag1[c]:
            copy.wait_recv()
        z = rows_of(pre, c) + mm(meanb[c].reshape(-1, h), n2)
        g = gate(z)
        s = z * g
        grad = (rows_of(cotg, c) * (g + s - s * g)).astype(BF16)
        mpart[c] = mm_nt(grad, n2).astype(BF16).reshape(blocks, chunk, h)
        rs2.append(scatter(mpart, mrecv, rs2_ss, rs2_rs, c))
        hiddenb[c] = s.astype(BF16).reshape(blocks, chunk, h)
        gradb[c] = grad.reshape(blocks, chunk, h)

    def add_weights(c, first, parts):
        for i, part in enumerate(parts):
            at = slice((first + i) * h, (first + i + 1) * h)
            wacc[at] = part if c == 0 else wacc[at] + part

    ag2 = []
    for c in range(CHUNKS):
        state = rows_of(state_ref, c)
        grad = gradb[c].reshape(-1, h)
        put_rows(fpart, c, mm_nt(grad, n1))
        put_rows(
            upd_ref,
            c,
            (state.astype(F32) + mm(hiddenb[c].reshape(-1, h), ns)).astype(BF16),
        )
        ag2.append(reduce_spread(rs2[c], mpart, mrecv, mgrad, ag2_ss, ag2_rs, c))
    back = []
    for c in range(CHUNKS):
        node_grad = gradb[c].reshape(-1, h)
        add_weights(
            c,
            0,
            (
                mm_tn(rows_of(state_ref, c), node_grad),
                mm_tn(fluxb[c].reshape(-1, h), node_grad),
                mm_tn(meanb[c].reshape(-1, h), node_grad),
                mm_tn(hiddenb[c].reshape(-1, h), rows_of(cot_ref, c)),
            ),
        )
        for copy in ag2[c]:
            copy.wait_recv()
        grad = (rows_of(fpart, c) + mgrad[c].reshape(-1, h).astype(F32)).astype(BF16)
        fgradb[c] = grad.reshape(blocks, chunk, h)
        wide = mm_nt(grad, es).reshape(blocks, chunk, h)
        gwsend[c] = wide[:BND].astype(BF16)
        back.append(
            [
                remote(
                    gwsend.at[c],
                    gwhalo.at[c, s],
                    back_ss.at[c * len(offs) + s],
                    back_rs.at[c * len(offs) + s],
                    dom_dev(n_dom - o),
                )
                for s, o in enumerate(offs)
            ]
        )
        gw[:blocks, c * chunk : (c + 1) * chunk] = wide
    for c in range(CHUNKS):
        add_weights(c, 4, (mm_tn(rows_of(nd, c).astype(BF16), fgradb[c].reshape(-1, h)),))

    def weights_out(first, count, got, sem):
        size = count // n_grp
        wsend[first : first + count] = wacc[first : first + count].astype(BF16)
        return [
            remote(
                wsend.at[pl.ds(pl.multiple_of(first + grp_id(k) * size, 16), size)],
                got.at[k - 1],
                wr_ss.at[sem, k - 1],
                wr_rs.at[sem, k - 1],
                grp_dev(k),
            )
            for k in range(1, n_grp)
        ]

    def weights_mid(copies, first, count, got, held, sem):
        size = count // n_grp
        for copy in copies:
            copy.wait_recv()
        total = wacc[pl.ds(pl.multiple_of(first + grp * size, 16), size)]
        for k in range(n_grp - 1):
            total = total + got[k].astype(F32)
        held[dom] = total.astype(BF16)
        return [
            remote(
                held.at[dom],
                held.at[dom],
                wd_ss.at[sem, o - 1],
                wd_rs.at[sem, o - 1],
                dom_dev(o),
            )
            for o in range(1, n_dom)
        ]

    def weights_in(copies, first, count, held, sem):
        size = count // n_grp
        for copy in copies:
            copy.wait_recv()
        total = held[0].astype(F32)
        for o in range(1, n_dom):
            total = total + held[o].astype(F32)
        mine = pl.ds(pl.multiple_of(first + grp * size, 16), size)
        wfin[mine] = total.astype(BF16)
        return [
            remote(
                wfin.at[mine],
                wfin.at[mine],
                wg_ss.at[sem, k - 1],
                wg_rs.at[sem, k - 1],
                grp_dev(k),
            )
            for k in range(1, n_grp)
        ]

    def spread_faces(start, faces, width, at, size, load):
        aa = [acc_a[b, pl.ds(at, size), :] if load else None for b in range(width)]
        bb = [acc_b[b, pl.ds(at, size), :] if load else None for b in range(width)]

        def put(total, term):
            return term if total is None else total + term

        for f, (ia, ic) in enumerate(faces):
            t = gw[ia, pl.ds(at, size), :] - gw[ic, pl.ds(at, size), :]
            p1 = t * slope[start + f, 0, pl.ds(at, size), :]
            p2 = t * slope[start + f, 1, pl.ds(at, size), :]
            for b in range(width):
                if load:
                    w = wo_s[f * width + b]
                    aa[b] = put(aa[b], w * p1)
                    bb[b] = put(bb[b], -w * p2)
                else:
                    wa, wc = wa_s[f * width + b], wc_s[f * width + b]
                    aa[b] = put(aa[b], wa * p1 - wc * p2)
                    bb[b] = put(bb[b], wc * p1 - wa * p2)
        for b in range(width):
            acc_a[b, pl.ds(at, size), :] = aa[b]
            acc_b[b, pl.ds(at, size), :] = bb[b]

    n_rows = 5 * h
    w1 = weights_out(0, n_rows, wrecv_n, 0)
    for c in range(CHUNKS):
        tiles(c, BWD_TILE, lambda at: spread_faces(0, inner_faces, blocks, at, BWD_TILE, False))
        if c == 0:
            w2 = weights_mid(w1, 0, n_rows, wrecv_n, wdom_n, 0)
    for c in range(CHUNKS):
        for copy in back[c]:
            copy.wait_recv()
        gw[blocks:, c * chunk : (c + 1) * chunk] = (
            gwhalo[c].reshape(-1, chunk, h).astype(F32)
        )
        tiles(c, BWD_TILE, lambda at: spread_faces(inner, outer, BND, at, BWD_TILE, True))
        a = rows_of(acc_a, c).astype(BF16)
        b = rows_of(acc_b, c).astype(BF16)
        state = rows_of(state_ref, c)
        add_weights(c, 5, (mm_tn(state, a), mm_tn(state, b)))
    e1 = weights_out(n_rows, 2 * h, wrecv_e, 1)
    w3 = weights_in(w2, 0, n_rows, wdom_n, 0)

    def finish(c):
        a = rows_of(acc_a, c).astype(BF16)
        b = rows_of(acc_b, c).astype(BF16)
        total = rows_of(cot_ref, c).astype(F32) + mm_nt(gradb[c].reshape(-1, h), n0)
        total = total + mm_nt(a, ef_ref[:h]) + mm_nt(b, ef_ref[h:])
        put_rows(sgrad_ref, c, total.astype(BF16))

    half = CHUNKS // 2
    for c in range(half):
        finish(c)
    e2 = weights_mid(e1, n_rows, 2 * h, wrecv_e, wdom_e, 1)
    for c in range(half, CHUNKS):
        finish(c)
    for copy in w3:
        copy.wait_recv()
    e3 = weights_in(e2, n_rows, 2 * h, wdom_e, 1)
    for group in [near_c] + halo_c + rs1 + ag1 + rs2 + ag2 + back + [w1, w2, w3, e1, e2]:
        for copy in group:
            copy.wait_send()
    for copy in e3:
        copy.wait()


def output_kernel(
    scale,
    upd_in,
    sgrad_in,
    w_any,
    upd_ref,
    sgrad_ref,
    efg_ref,
    esg_ref,
    nfg_ref,
    nsg_ref,
    w_in,
    load_s,
):
    h = upd_in.shape[2]
    pairs = ((w_any, w_in), (upd_in, upd_ref), (sgrad_in, sgrad_ref))
    loads = [
        pltpu.make_async_copy(src, dst, load_s.at[i]) for i, (src, dst) in enumerate(pairs)
    ]
    for load in loads:
        load.start()
    loads[0].wait()
    nfg_ref[...] = w_in[: 3 * h].astype(F32) * scale
    nsg_ref[...] = w_in[3 * h : 4 * h].astype(F32) * scale
    esg_ref[...] = w_in[4 * h : 5 * h].astype(F32) * scale
    efg_ref[...] = w_in[5 * h :].astype(F32) * scale
    for load in loads[1:]:
        load.wait()


def shards(
    node_state,
    state_cotangent,
    edge_first,
    edge_second,
    node_first,
    node_second,
    inner_count,
    inner_pairs,
    outer_pairs,
):
    state = node_state[0, 0]
    cot = state_cotangent[0, 0]
    blocks, rows, h = state.shape
    n_dom, n_lev, n_mem = (lax.axis_size(x) for x in ("dom", "lev", "mem"))
    n_grp = n_lev * n_mem
    inner = inner_pairs.shape[0]
    outer = outer_pairs.shape[0]
    per = outer // REACH
    offs = sorted({s * o % n_dom for o in range(1, REACH + 1) for s in (1, -1)})
    scale = 1.0 / math.sqrt(n_mem * n_lev * blocks * n_dom * rows)
    faces = inner + 2 * outer
    chunk = rows // CHUNKS
    share = blocks // n_lev
    slots = len(offs)
    table = blocks + BND * slots
    size_n = 5 * h // n_grp
    size_e = 2 * h // n_grp
    dma = pltpu.SemaphoreType.DMA
    lev_sems = [dma((CHUNKS * (n_lev - 1),))] * 8
    full = (blocks, rows, h)
    cut = (CHUNKS, blocks, chunk, h)
    smem = pl.BlockSpec(memory_space=pltpu.SMEM)
    vmem = pl.BlockSpec(memory_space=pltpu.VMEM)
    held = pl.pallas_call(
        functools.partial(layer_kernel, (n_dom, n_lev, n_mem), offs),
        out_shape=(
            jax.ShapeDtypeStruct(full, BF16),
            jax.ShapeDtypeStruct(full, BF16),
            jax.ShapeDtypeStruct((7 * h, h), BF16),
        ),
        in_specs=[smem] * 3 + [pl.BlockSpec(memory_space=pl.ANY)] * 6,
        out_specs=(vmem,) * 3,
        scratch_shapes=[
            pltpu.SMEM((REACH, 2, outer), jnp.int32),
            pltpu.SMEM((inner * blocks,), F32),
            pltpu.SMEM((inner * blocks,), F32),
            pltpu.SMEM((inner * blocks,), F32),
            pltpu.SMEM((2 * outer * BND,), F32),
            pltpu.VMEM((CHUNKS, slots, BND, chunk, h), BF16),
            pltpu.VMEM((table, rows, 2 * h), F32),
            pltpu.VMEM((faces, 2, rows, h), F32),
            pltpu.VMEM(full, F32),
            pltpu.VMEM(cut, BF16),
            pltpu.VMEM((CHUNKS, n_lev - 1, share, chunk, h), BF16),
            pltpu.VMEM(cut, BF16),
            pltpu.VMEM(full, F32),
            pltpu.VMEM(full, F32),
            pltpu.VMEM(cut, BF16),
            pltpu.VMEM(cut, BF16),
            pltpu.VMEM(cut, BF16),
            pltpu.VMEM(cut, BF16),
            pltpu.VMEM((CHUNKS, n_lev - 1, share, chunk, h), BF16),
            pltpu.VMEM(cut, BF16),
            pltpu.VMEM(full, F32),
            pltpu.VMEM((table, rows, h), F32),
            pltpu.VMEM((CHUNKS, BND, chunk, h), BF16),
            pltpu.VMEM((CHUNKS, slots, BND, chunk, h), BF16),
            pltpu.VMEM(full, F32),
            pltpu.VMEM(full, F32),
            pltpu.VMEM((7 * h, h), F32),
            pltpu.VMEM((7 * h, h), BF16),
            pltpu.VMEM((n_grp - 1, size_n, h), BF16),
            pltpu.VMEM((n_grp - 1, size_e, h), BF16),
            pltpu.VMEM((n_dom, size_n, h), BF16),
            pltpu.VMEM((n_dom, size_e, h), BF16),
            dma((CHUNKS * slots,)),
            dma((CHUNKS * slots,)),
            *lev_sems,
            dma((CHUNKS * slots,)),
            dma((CHUNKS * slots,)),
            dma((2, n_grp - 1)),
            dma((2, n_grp - 1)),
            dma((2, n_dom - 1)),
            dma((2, n_dom - 1)),
            dma((2, n_grp - 1)),
            dma((2, n_grp - 1)),
            dma((REACH,)),
            dma((REACH,)),
            pltpu.VMEM(full, BF16),
            pltpu.VMEM(full, BF16),
            pltpu.VMEM((2 * h, h), BF16),
            pltpu.VMEM((h, h), BF16),
            pltpu.VMEM((3 * h, h), BF16),
            pltpu.VMEM((h, h), BF16),
            dma((6,)),
        ],
        compiler_params=pltpu.CompilerParams(
            collective_id=0, has_side_effects=True, vmem_limit_bytes=56 * 1024 * 1024
        ),
    )(
        inner_count,
        inner_pairs.T,
        outer_pairs.T,
        state,
        cot,
        edge_first,
        edge_second,
        node_first,
        node_second,
    )
    upd, sgrad, efg, esg, nfg, nsg = pl.pallas_call(
        functools.partial(output_kernel, scale),
        out_shape=(
            jax.ShapeDtypeStruct(full, BF16),
            jax.ShapeDtypeStruct(full, BF16),
            jax.ShapeDtypeStruct((2 * h, h), F32),
            jax.ShapeDtypeStruct((h, h), F32),
            jax.ShapeDtypeStruct((3 * h, h), F32),
            jax.ShapeDtypeStruct((h, h), F32),
        ),
        in_specs=[pl.BlockSpec(memory_space=pl.ANY)] * 3,
        out_specs=(vmem,) * 6,
        scratch_shapes=[pltpu.VMEM((7 * h, h), BF16), dma((3,))],
        compiler_params=pltpu.CompilerParams(vmem_limit_bytes=60 * 1024 * 1024),
    )(*held)
    return (upd[None, None], sgrad[None, None], efg, esg, nfg, nsg)


def solution(mesh):
    data = P("mem", "lev", "dom", None, None)
    return jax.shard_map(
        shards,
        mesh=mesh,
        in_specs=(data, data, P(), P(), P(), P(), P("dom"), P("dom", None), P("dom", None)),
        out_specs=(data, data, P(), P(), P(), P()),
        check_vma=False,
    )
```
